32 devices in a mesh: layer: 8 (over z, x), shard: 4 (over y, core).
Axes of the slice: x: 2, y: 2, z: 4, core: 2. Of those that a mesh axis runs over, the one named last changes fastest.
Arguments:
- gate_grad: bfloat16 [8, 2048, 512], P('layer', 'shard'), parts along dimension 0, may hold values from -400 to 400
- gate_moment: bfloat16 [8, 2048, 512], P('layer', 'shard'), parts along dimension 0, may hold values from -120 to 120
- down_grad: bfloat16 [8, 2048, 512], P('layer', 'shard'), parts along dimension 0, may hold values from -400 to 400
- down_moment: bfloat16 [8, 2048, 512], P('layer', 'shard'), parts along dimension 0, may hold values from -120 to 120
Outputs:
- gate_update: bfloat16 [8, 2048, 512], P('layer', 'shard'), parts along dimension 0
- down_update: bfloat16 [8, 2048, 512], P('layer', 'shard'), parts along dimension 0
The draws below stay inside these ranges and needn't reach their ends.
There are 8 independent parts, one for each index of `layer`. The reference program is written for one: setup_inputs(seed, part) draws one part's arguments, and reference() takes and returns one part's arrays. A program takes and returns all parts, laid end to end along the dimension named above; each array names one. Nothing has to cross between parts.
All inputs are finite; a program needn't handle non-finite values.
Results may differ from the reference program's by a relative error of at most 0.0068.
Values may be sent and summed in bfloat16 or wider, within the bound.
A program may use at most 64 MiB of HBM per device.

```python
import math
import jax
import jax.numpy as jnp
from jax import lax

D = 2048
FF = 512
ITERS = 2
EXPERTS = 1
N_SHARD = 4


def scaled_field(key):
    keys = jax.random.split(key, 3)
    row_scale = jnp.exp(jax.random.uniform(keys[0], (EXPERTS, D, 1), jnp.float32, 0.0, math.log(10.0)))
    column_scale = jnp.exp(jax.random.uniform(keys[1], (EXPERTS, 1, FF), jnp.float32, 0.0, math.log(10.0)))
    entries = jax.random.truncated_normal(keys[2], -4.0, 4.0, (EXPERTS, D, FF), jnp.float32)
    return (entries * row_scale * column_scale).astype(jnp.bfloat16)


def draw_gate_grad(key, part):
    return scaled_field(jax.random.fold_in(key, 11))


def draw_down_grad(key, part):
    return scaled_field(jax.random.fold_in(key, 23))


def block_scale(key, shape, cuts, least, high):
    level, own = 1.0, jax.random.fold_in(key, 6)
    for axis_at, parts in cuts:
        heights = jnp.exp(jax.random.uniform(jax.random.fold_in(own, axis_at), (parts,), jnp.float32, least / len(cuts), high / len(cuts)))
        level = level * jnp.repeat(heights, shape[axis_at] // parts).reshape([-1 if axis == axis_at else 1 for axis in range(len(shape))])
    return level


def scatter_about(stream_key, shape, spread, limit, pieces=(), kind=jnp.bfloat16):
    gain = block_scale(stream_key, shape, pieces, -0.22, 0.18) if pieces else 1.0
    values = jax.random.normal(stream_key, shape, jnp.float32) * spread * gain
    return jnp.minimum(jnp.maximum(values, -limit), limit).astype(kind)


def setup_inputs(seed: int = 0, part: int = 0) -> dict:
    splits = jax.random.split(jax.random.key(seed), 5)
    own_keys = jax.random.split(jax.random.fold_in(splits[4], part), 5)
    gate_grad = draw_gate_grad(jax.random.fold_in(jax.random.fold_in(splits[4], part), 71), part)
    gate_moment = scatter_about(own_keys[1], (EXPERTS, D, FF), 20.0, 120.0, ((1, 4),))
    down_grad = draw_down_grad(jax.random.fold_in(jax.random.fold_in(splits[4], part), 71), part)
    down_moment = scatter_about(own_keys[3], (EXPERTS, D, FF), 20.0, 120.0, ((1, 4),))
    return dict(gate_grad=gate_grad, gate_moment=gate_moment, down_grad=down_grad, down_moment=down_moment)


MOMENTUM_RATE = 0.95
COEF_A = 3.4445
COEF_B = -4.775
COEF_C = 2.0315
EPSILON = 1e-07

def blended(gradient, moment):
    buffer = MOMENTUM_RATE * moment.astype(jnp.float32) + gradient.astype(jnp.float32)
    return (gradient.astype(jnp.float32) + MOMENTUM_RATE * buffer).astype(jnp.bfloat16)

def transposed_product(first_matrix, second_matrix):
    return lax.dot_general(first_matrix.astype(jnp.float32), second_matrix.astype(jnp.float32), (((0,), (0,)), ((), ())), preferred_element_type=jnp.float32)

def quintic(current):
    square = jnp.dot(current, current, preferred_element_type=jnp.float32)
    identity = jnp.eye(current.shape[0], dtype=jnp.float32)
    return (COEF_A * identity + COEF_B * current.astype(jnp.float32) + COEF_C * square).astype(jnp.bfloat16)

def orthogonal_update(matrix):
    blocks = matrix.reshape(N_SHARD, 4, D // (4 * N_SHARD), FF)
    total = jnp.zeros((FF, FF), jnp.float32)
    for member in range(4):
        quarter = blocks[:, member].reshape(-1, FF)
        partial_value = lax.optimization_barrier(transposed_product(quarter, quarter).astype(jnp.bfloat16))
        total = total + partial_value.astype(jnp.float32)
    factor = 1.0 / (jnp.sqrt(jnp.trace(total)) + EPSILON)
    scaled = (total * (factor * factor)).astype(jnp.bfloat16)
    combined = quintic(scaled)
    for iteration in range(ITERS - 1):
        product = jnp.dot(scaled, combined, preferred_element_type=jnp.float32).astype(jnp.bfloat16)
        current = transposed_product(combined, product).astype(jnp.bfloat16)
        combined = jnp.dot(combined, quintic(current), preferred_element_type=jnp.float32).astype(jnp.bfloat16)
    result = jnp.dot(matrix, combined, preferred_element_type=jnp.float32) * (math.sqrt(D) * factor)
    return result.astype(jnp.bfloat16)

def reference(gate_grad, gate_moment, down_grad, down_moment):
    gate_input = blended(gate_grad, gate_moment)
    down_input = blended(down_grad, down_moment)
    gate_update = lax.map(orthogonal_update, gate_input)
    down_update = lax.map(orthogonal_update, down_input)
    return (gate_update, down_update)
```

```python
import functools
import math

import jax
import jax.numpy as jnp
from jax import lax
from jax.experimental import pallas as pl
from jax.experimental.pallas import tpu as pltpu
from jax.sharding import PartitionSpec as P

MOMENTUM_RATE = 0.95
COEF_A = 3.4445
COEF_B = -4.775
COEF_C = 2.0315
EPSILON = 1e-07
MESH = pl.DeviceIdType.MESH
BLOCK = 128
BF16 = jnp.bfloat16
F32 = jnp.float32


def blended(gradient, moment):
    buffer = MOMENTUM_RATE * moment.astype(F32) + gradient.astype(F32)
    return (gradient.astype(F32) + MOMENTUM_RATE * buffer).astype(BF16)


def product(first, second):
    return jnp.dot(first, second, preferred_element_type=F32)


def transposed_product(first, second):
    return lax.dot_general(first, second, (((0,), (0,)), ((), ())), preferred_element_type=F32)


def quintic(current, square):
    rows, columns = square.shape
    on_diagonal = lax.broadcasted_iota(jnp.int32, (rows, columns), 0) == lax.broadcasted_iota(
        jnp.int32, (rows, columns), 1
    )
    return jnp.where(on_diagonal, COEF_A, 0.0) + COEF_B * current.astype(F32) + COEF_C * square


def each(count, body):
    if count == 1:
        body(0)
    else:
        pl.loop(0, count)(body)


def kernel(
    shards,
    full_rows,
    gate_grad,
    gate_moment,
    down_grad,
    down_moment,
    out,
    inputs,
    blend,
    total,
    near_send,
    near_recv,
    far_send,
    far_recv,
    scaled_ref,
    combined_ref,
    other_ref,
    polished,
    input_sem,
    near_sems,
    far_sems,
    polished_sems,
):
    _, experts, rows, width = inputs.shape[1:]
    stages = shards.bit_length() - 2
    blocks = width // BLOCK
    me = lax.axis_index("shard")
    core = lax.rem(me, 2)
    near = me + 1 - 2 * core
    gate_slot, down_slot = 1 - core, core

    def far(stage):
        bit = lax.rem(me // (2 << stage), 2)
        return me + (1 - 2 * bit) * (2 << stage)

    loads = []
    for slot, pair in ((gate_slot, (gate_grad, gate_moment)), (down_slot, (down_grad, down_moment))):
        for member, source in enumerate(pair):
            loads.append(
                pltpu.make_async_copy(source, inputs.at[slot, member], input_sem.at[slot, member])
            )
    for load in loads:
        load.start()

    barrier = pltpu.get_barrier_semaphore()
    for peer in [near] + [far(stage) for stage in range(stages)]:
        pl.semaphore_signal(barrier, inc=1, device_id={"shard": peer}, device_id_type=MESH)

    def wait_loads(slot):
        for member in range(2):
            pltpu.make_async_copy(
                gate_grad, inputs.at[slot, member], input_sem.at[slot, member]
            ).wait()

    def upper(block):
        return pl.ds(block * BLOCK, BLOCK), pl.ds(block * BLOCK, width - block * BLOCK)

    def near_copy(expert, block):
        row, column = upper(block)
        return pltpu.make_async_remote_copy(
            src_ref=near_send.at[expert, row, column],
            dst_ref=near_recv.at[expert, row, column],
            send_sem=near_sems.at[0, expert, block],
            recv_sem=near_sems.at[1, expert, block],
            device_id={"shard": near},
            device_id_type=MESH,
        )

    def far_copy(stage, expert, block):
        row, column = upper(block)
        return pltpu.make_async_remote_copy(
            src_ref=far_send.at[expert, row, column],
            dst_ref=far_recv.at[stage, expert, row, column],
            send_sem=far_sems.at[0, stage, expert, block],
            recv_sem=far_sems.at[1, stage, expert, block],
            device_id={"shard": far(stage)},
            device_id_type=MESH,
        )

    def polished_copy(expert, block):
        row = pl.ds(block * BLOCK, BLOCK)
        return pltpu.make_async_remote_copy(
            src_ref=polished.at[1, expert, row],
            dst_ref=polished.at[0, expert, row],
            send_sem=polished_sems.at[0, expert, block],
            recv_sem=polished_sems.at[1, expert, block],
            device_id={"shard": near},
            device_id_type=MESH,
        )

    def blend_slot(slot, expert):
        blend[slot, expert] = blended(inputs[slot, 0, expert], inputs[slot, 1, expert])

    def gram(slot, expert, block):
        row, column = upper(block)
        return transposed_product(blend[slot, expert, :, row], blend[slot, expert, :, column])

    wait_loads(0)
    each(experts, lambda expert: blend_slot(0, expert))
    pl.semaphore_wait(barrier, 1 + stages)

    def send_other(expert):
        for block in range(blocks):
            row, column = upper(block)
            near_send[expert, row, column] = gram(0, expert, block).astype(BF16)
            near_copy(expert, block).start()

    each(experts, send_other)
    wait_loads(1)
    each(experts, lambda expert: blend_slot(1, expert))

    def own_total(expert):
        for block in range(blocks):
            row, column = upper(block)
            total[expert, row, column] = gram(1, expert, block)

    each(experts, own_total)

    def gather_near(expert):
        for block in range(blocks):
            row, column = upper(block)
            near_copy(expert, block).wait_recv()
            held = total[expert, row, column] + near_recv[expert, row, column].astype(F32)
            total[expert, row, column] = held
            if stages:
                far_send[expert, row, column] = held.astype(BF16)
                far_copy(0, expert, block).start()

    each(experts, gather_near)

    for stage in range(stages):
        if stage:

            def send_far(expert, stage=stage):
                for block in range(blocks):
                    row, column = upper(block)
                    far_copy(stage - 1, expert, block).wait_send()
                    far_send[expert, row, column] = total[expert, row, column].astype(BF16)
                    far_copy(stage, expert, block).start()

            each(experts, send_far)

        def gather_far(expert, stage=stage):
            for block in range(blocks):
                row, column = upper(block)
                far_copy(stage, expert, block).wait_recv()
                total[expert, row, column] = total[expert, row, column] + far_recv[
                    stage, expert, row, column
                ].astype(F32)

        each(experts, gather_far)

    def polish(expert):
        on_diagonal = lax.broadcasted_iota(jnp.int32, (BLOCK, BLOCK), 0) == lax.broadcasted_iota(
            jnp.int32, (BLOCK, BLOCK), 1
        )
        diagonal = jnp.zeros((BLOCK, BLOCK), F32)
        for block in range(blocks):
            row = pl.ds(block * BLOCK, BLOCK)
            diagonal = diagonal + jnp.where(on_diagonal, total[expert, row, row], 0.0)
        trace = jnp.sum(diagonal, axis=(0, 1), keepdims=True)
        factor = 1.0 / (jnp.sqrt(trace) + EPSILON)
        for block in range(blocks):
            row, column = upper(block)
            strip = (total[expert, row, column] * (factor * factor)).astype(BF16)
            scaled_ref[row, column] = strip
            for later in range(block + 1, blocks):
                start = (later - block) * BLOCK
                scaled_ref[pl.ds(later * BLOCK, BLOCK), row] = strip[:, start : start + BLOCK].T
        scaled = scaled_ref[...]
        combined_ref[...] = quintic(scaled, product(scaled, scaled)).astype(BF16)
        combined = combined_ref[...]
        other_ref[...] = product(scaled, combined).astype(BF16)
        scaled_ref[...] = product(combined, other_ref[...]).astype(BF16)
        current = scaled_ref[...]
        other_ref[...] = quintic(current, product(current, current)).astype(BF16)
        gain = math.sqrt(full_rows) * factor
        for block in range(blocks):
            row = pl.ds(block * BLOCK, BLOCK)
            polished[1, expert, row] = (product(combined_ref[row], other_ref[...]) * gain).astype(BF16)
            polished_copy(expert, block).start()

    each(experts, polish)

    def own_update(expert):
        out[core, expert] = product(blend[1, expert], polished[1, expert]).astype(BF16)

    each(experts, own_update)

    def other_update(expert):
        for block in range(blocks):
            polished_copy(expert, block).wait_recv()
        out[1 - core, expert] = product(blend[0, expert], polished[0, expert]).astype(BF16)

    each(experts, other_update)

    def drain(expert):
        for block in range(blocks):
            near_copy(expert, block).wait_send()
            if stages:
                far_copy(stages - 1, expert, block).wait_send()
            polished_copy(expert, block).wait_send()

    each(experts, drain)


def updates(shards, gate_grad, gate_moment, down_grad, down_moment):
    experts, rows, width = gate_grad.shape
    stages = max(shards.bit_length() - 2, 1)
    blocks = width // BLOCK
    out = pl.pallas_call(
        functools.partial(kernel, shards, rows * shards),
        out_shape=jax.ShapeDtypeStruct((2, experts, rows, width), BF16),
        in_specs=[pl.BlockSpec(memory_space=pl.ANY)] * 4,
        out_specs=pl.BlockSpec(memory_space=pltpu.VMEM),
        scratch_shapes=[
            pltpu.VMEM((2, 2, experts, rows, width), BF16),
            pltpu.VMEM((2, experts, rows, width), BF16),
            pltpu.VMEM((experts, width, width), F32),
            pltpu.VMEM((experts, width, width), BF16),
            pltpu.VMEM((experts, width, width), BF16),
            pltpu.VMEM((experts, width, width), BF16),
            pltpu.VMEM((stages, experts, width, width), BF16),
            pltpu.VMEM((width, width), BF16),
            pltpu.VMEM((width, width), BF16),
            pltpu.VMEM((width, width), BF16),
            pltpu.VMEM((2, experts, width, width), BF16),
            pltpu.SemaphoreType.DMA((2, 2)),
            pltpu.SemaphoreType.DMA((2, experts, blocks)),
            pltpu.SemaphoreType.DMA((2, stages, experts, blocks)),
            pltpu.SemaphoreType.DMA((2, experts, blocks)),
        ],
        compiler_params=pltpu.CompilerParams(collective_id=0, has_side_effects=True),
    )(gate_grad, gate_moment, down_grad, down_moment)
    return out[0], out[1]


def solution(mesh):
    placed = P("layer", "shard", None)
    return jax.shard_map(
        functools.partial(updates, mesh.shape["shard"]),
        mesh=mesh,
        in_specs=(placed,) * 4,
        out_specs=(placed,) * 2,
        check_vma=False,
    )
```

```python
import functools
import math

import jax
import jax.numpy as jnp
from jax import lax
from jax.experimental import pallas as pl
from jax.experimental.pallas import tpu as pltpu
from jax.sharding import PartitionSpec as P

MOMENTUM_RATE = 0.95
COEF_A = 3.4445
COEF_B = -4.775
COEF_C = 2.0315
EPSILON = 1e-07
MESH = pl.DeviceIdType.MESH
BLOCK = 128
EXTRA = 16
BF16 = jnp.bfloat16
F32 = jnp.float32


def blended(gradient, moment):
    buffer = MOMENTUM_RATE * moment.astype(F32) + gradient.astype(F32)
    return (gradient.astype(F32) + MOMENTUM_RATE * buffer).astype(BF16)


def product(first, second):
    return jnp.dot(first, second, preferred_element_type=F32)


def transposed_product(first, second):
    return lax.dot_general(first, second, (((0,), (0,)), ((), ())), preferred_element_type=F32)


def iotas(size):
    return tuple(lax.broadcasted_iota(jnp.int32, (size, size), axis) for axis in range(2))


def quintic(current, square):
    row_at, column_at = iotas(square.shape[0])
    return jnp.where(row_at == column_at, COEF_A, 0.0) + COEF_B * current.astype(F32) + COEF_C * square


def each(count, body):
    if count == 1:
        body(0)
    else:
        pl.loop(0, count)(body)


def kernel(
    shards,
    full_rows,
    gate_grad,
    gate_moment,
    down_grad,
    down_moment,
    out,
    inputs,
    blend,
    total,
    first_ref,
    near_send,
    near_recv,
    far_send,
    far_recv,
    scaled_ref,
    combined_ref,
    other_ref,
    polished,
    input_sem,
    near_sems,
    far_sems,
    polished_sems,
):
    _, experts, rows, width = inputs.shape[1:]
    stages = shards.bit_length() - 2
    blocks, half = width // BLOCK, width // 2
    me = lax.axis_index("shard")
    core = lax.rem(me, 2)
    near = me + 1 - 2 * core

    def far(stage):
        bit = lax.rem(me // (2 << stage), 2)
        return me + (1 - 2 * bit) * (2 << stage)

    def load(slot, pair):
        for member, source in enumerate(pair):
            pltpu.make_async_copy(source, inputs.at[slot, member], input_sem.at[slot, member]).start()

    @pl.when(core == 0)
    def _():
        load(0, (down_grad, down_moment))
        load(1, (gate_grad, gate_moment))

    @pl.when(core == 1)
    def _():
        load(0, (gate_grad, gate_moment))
        load(1, (down_grad, down_moment))

    barrier = pltpu.get_barrier_semaphore()
    for peer in [near] + [far(stage) for stage in range(stages)]:
        pl.semaphore_signal(barrier, inc=1, device_id={"shard": peer}, device_id_type=MESH)

    def wait_loads(slot):
        for member in range(2):
            pltpu.make_async_copy(
                gate_grad, inputs.at[slot, member], input_sem.at[slot, member]
            ).wait()

    def part(block):
        return pl.ds(block * BLOCK, BLOCK + (EXTRA if block == blocks - 1 else 0))

    def near_copy(expert, block):
        row = part(block)
        return pltpu.make_async_remote_copy(
            src_ref=near_send.at[expert, row],
            dst_ref=near_recv.at[expert, row],
            send_sem=near_sems.at[0, expert, block],
            recv_sem=near_sems.at[1, expert, block],
            device_id={"shard": near},
            device_id_type=MESH,
        )

    def far_copy(stage, expert, block):
        row = part(block)
        return pltpu.make_async_remote_copy(
            src_ref=far_send.at[expert, row],
            dst_ref=far_recv.at[stage, expert, row],
            send_sem=far_sems.at[0, stage, expert, block],
            recv_sem=far_sems.at[1, stage, expert, block],
            device_id={"shard": far(stage)},
            device_id_type=MESH,
        )

    def polished_copy(expert, block):
        row = pl.ds(block * BLOCK, BLOCK)
        return pltpu.make_async_remote_copy(
            src_ref=polished.at[1, expert, row],
            dst_ref=polished.at[0, expert, row],
            send_sem=polished_sems.at[0, expert, block],
            recv_sem=polished_sems.at[1, expert, block],
            device_id={"shard": near},
            device_id_type=MESH,
        )

    def blend_slot(slot, expert):
        blend[slot, expert] = blended(inputs[slot, 0, expert], inputs[slot, 1, expert])

    def packed_gram(slot, expert, target, ready):
        matrix = blend[slot, expert]
        for block in range(blocks // 2):
            row = pl.ds(block * BLOCK, BLOCK)
            strip = transposed_product(matrix[:, block * BLOCK : (block + 1) * BLOCK], matrix)
            target[expert, row] = strip[:, half:].astype(target.dtype)
            ready(expert, block)
            first_ref[row] = strip[:, :half]
        last = transposed_product(matrix[:, half:], matrix[:, half:])
        row_at, column_at = iotas(half)
        target[expert, pl.ds(half, half)] = jnp.where(row_at <= column_at, first_ref[...], last).astype(
            target.dtype
        )
        diagonal = jnp.sum(jnp.where(row_at == column_at, last, 0.0), axis=0, keepdims=True)
        target[expert, pl.ds(width, EXTRA)] = jnp.broadcast_to(diagonal, (EXTRA, half)).astype(
            target.dtype
        )
        for block in range(blocks // 2, blocks):
            ready(expert, block)

    wait_loads(0)
    each(experts, lambda expert: blend_slot(0, expert))
    pl.semaphore_wait(barrier, 1 + stages)
    each(
        experts,
        lambda expert: packed_gram(
            0, expert, near_send, lambda at, block: near_copy(at, block).start()
        ),
    )
    wait_loads(1)
    each(experts, lambda expert: blend_slot(1, expert))
    each(experts, lambda expert: packed_gram(1, expert, total, lambda at, block: None))

    def gather_near(expert):
        for block in range(blocks):
            row = part(block)
            near_copy(expert, block).wait_recv()
            held = total[expert, row] + near_recv[expert, row].astype(F32)
            total[expert, row] = held
            if stages:
                far_send[expert, row] = held.astype(BF16)
                far_copy(0, expert, block).start()

    each(experts, gather_near)

    for stage in range(stages):
        if stage:

            def send_far(expert, stage=stage):
                for block in range(blocks):
                    row = part(block)
                    far_copy(stage - 1, expert, block).wait_send()
                    far_send[expert, row] = total[expert, row].astype(BF16)
                    far_copy(stage, expert, block).start()

            each(experts, send_far)

        def gather_far(expert, stage=stage):
            for block in range(blocks):
                row = part(block)
                far_copy(stage, expert, block).wait_recv()
                total[expert, row] = total[expert, row] + far_recv[stage, expert, row].astype(F32)

        each(experts, gather_far)

    def polish(expert):
        row_at, column_at = iotas(half)
        packed = total[expert, pl.ds(half, half)]
        diagonal = total[expert, pl.ds(width, 1)]
        kept = jnp.where(row_at == column_at, packed, 0.0)
        trace = jnp.sum(jnp.sum(kept, axis=0, keepdims=True) + diagonal, axis=1, keepdims=True)
        factor = 1.0 / (jnp.sqrt(trace) + EPSILON)
        square = factor * factor
        upper, lower = pl.ds(0, half), pl.ds(half, half)
        side = (total[expert, upper] * square).astype(BF16)
        scaled_ref[upper, lower] = side
        scaled_ref[lower, upper] = side.T
        packed = packed * square
        flipped = packed.T
        scaled_ref[upper, upper] = jnp.where(row_at <= column_at, packed, flipped).astype(BF16)
        scaled_ref[lower, lower] = jnp.where(
            row_at == column_at,
            diagonal * square,
            jnp.where(row_at > column_at, packed, flipped),
        ).astype(BF16)
        scaled = scaled_ref[...]
        combined_ref[...] = quintic(scaled, product(scaled, scaled)).astype(BF16)
        combined = combined_ref[...]
        other_ref[...] = product(scaled, combined).astype(BF16)
        scaled_ref[...] = product(combined, other_ref[...]).astype(BF16)
        current = scaled_ref[...]
        other_ref[...] = quintic(current, product(current, current)).astype(BF16)
        gain = math.sqrt(full_rows) * factor
        for block in range(blocks):
            row = pl.ds(block * BLOCK, BLOCK)
            polished[1, expert, row] = (product(combined_ref[row], other_ref[...]) * gain).astype(BF16)
            polished_copy(expert, block).start()

    each(experts, polish)

    def own_update(expert):
        out[core, expert] = product(blend[1, expert], polished[1, expert]).astype(BF16)

    each(experts, own_update)

    def other_update(expert):
        for block in range(blocks):
            polished_copy(expert, block).wait_recv()
        out[1 - core, expert] = product(blend[0, expert], polished[0, expert]).astype(BF16)

    each(experts, other_update)

    def drain(expert):
        for block in range(blocks):
            near_copy(expert, block).wait_send()
            if stages:
                far_copy(stages - 1, expert, block).wait_send()
            polished_copy(expert, block).wait_send()

    each(experts, drain)


def updates(shards, gate_grad, gate_moment, down_grad, down_moment):
    experts, rows, width = gate_grad.shape
    stages = max(shards.bit_length() - 2, 1)
    blocks = width // BLOCK
    packed = (width + EXTRA, width // 2)
    limit = experts * (24 * rows * width + (16 + 2 * stages) * width * width) + (16 << 20)
    out = pl.pallas_call(
        functools.partial(kernel, shards, rows * shards),
        out_shape=pltpu.VMEM((2, experts, rows, width), BF16),
        in_specs=[pl.BlockSpec(memory_space=pltpu.HBM)] * 4,
        out_specs=pl.BlockSpec(memory_space=pltpu.VMEM),
        scratch_shapes=[
            pltpu.VMEM((2, 2, experts, rows, width), BF16),
            pltpu.VMEM((2, experts, rows, width), BF16),
            pltpu.VMEM((experts, *packed), F32),
            pltpu.VMEM((width // 2, width // 2), F32),
            pltpu.VMEM((experts, *packed), BF16),
            pltpu.VMEM((experts, *packed), BF16),
            pltpu.VMEM((experts, *packed), BF16),
            pltpu.VMEM((stages, experts, *packed), BF16),
            pltpu.VMEM((width, width), BF16),
            pltpu.VMEM((width, width), BF16),
            pltpu.VMEM((width, width), BF16),
            pltpu.VMEM((2, experts, width, width), BF16),
            pltpu.SemaphoreType.DMA((2, 2)),
            pltpu.SemaphoreType.DMA((2, experts, blocks)),
            pltpu.SemaphoreType.DMA((2, stages, experts, blocks)),
            pltpu.SemaphoreType.DMA((2, experts, blocks)),
        ],
        compiler_params=pltpu.CompilerParams(collective_id=0, has_side_effects=True, vmem_limit_bytes=min(limit, 56 << 20)
        ),
    )(
        *(
            pltpu.with_memory_space_constraint(source, pltpu.HBM)
            for source in (gate_grad, gate_moment, down_grad, down_moment)
        )
    )
    return out[0], out[1]


def solution(mesh):
    placed = P("layer", "shard", None)
    return jax.shard_map(
        functools.partial(updates, mesh.shape["shard"]),
        mesh=mesh,
        in_specs=(placed,) * 4,
        out_specs=(placed,) * 2,
        check_vma=False,
    )
```

```python
import functools
import math

import jax
import jax.numpy as jnp
from jax import lax
from jax.experimental import pallas as pl
from jax.experimental.pallas import tpu as pltpu
from jax.sharding import PartitionSpec as P

MOMENTUM_RATE = 0.95
COEF_A = 3.4445
COEF_B = -4.775
COEF_C = 2.0315
EPSILON = 1e-07
MESH = pl.DeviceIdType.MESH
BLOCK = 128
EXTRA = 16
BF16 = jnp.bfloat16
F32 = jnp.float32


def blended(gradient, moment):
    buffer = MOMENTUM_RATE * moment.astype(F32) + gradient.astype(F32)
    return (gradient.astype(F32) + MOMENTUM_RATE * buffer).astype(BF16)


def product(first, second):
    return jnp.dot(first, second, preferred_element_type=F32)


def transposed_product(first, second):
    return lax.dot_general(first, second, (((0,), (0,)), ((), ())), preferred_element_type=F32)


def iotas(size):
    return tuple(lax.broadcasted_iota(jnp.int32, (size, size), axis) for axis in range(2))


def quintic(current, square, start):
    row_at, column_at = (lax.broadcasted_iota(jnp.int32, square.shape, axis) for axis in range(2))
    return jnp.where(row_at + start == column_at, COEF_A, 0.0) + COEF_B * current.astype(F32) + COEF_C * square


def each(count, body):
    if count == 1:
        body(0)
    else:
        pl.loop(0, count)(body)


def kernel(
    shards,
    full_rows,
    gate_grad,
    gate_moment,
    down_grad,
    down_moment,
    own_out,
    other_half,
    other_second,
    inputs,
    blend,
    total,
    near_send,
    near_recv,
    far_send,
    far_recv,
    scaled_ref,
    first,
    first_other,
    second,
    current_ref,
    input_sem,
    near_sems,
    far_sems,
    polished_sems,
):
    _, experts, rows, width = inputs.shape[1:]
    stages = shards.bit_length() - 2
    blocks, strips, half = width // BLOCK, width // BLOCK // 2, width // 2
    me = lax.axis_index("shard")
    core = lax.rem(me, 2)
    near = me + 1 - 2 * core

    def far(stage):
        bit = lax.rem(me // (2 << stage), 2)
        return me + (1 - 2 * bit) * (2 << stage)

    barrier = pltpu.get_barrier_semaphore()
    for peer in [far(stage) for stage in range(stages)] + [near]:
        pl.semaphore_signal(barrier, inc=1, device_id={"shard": peer}, device_id_type=MESH)

    def load(slot, pair):
        for member, source in enumerate(pair):
            pltpu.make_async_copy(source, inputs.at[slot, member], input_sem.at[slot, member]).start()

    @pl.when(core == 0)
    def _():
        load(0, (down_grad, down_moment))
        load(1, (gate_grad, gate_moment))

    @pl.when(core == 1)
    def _():
        load(0, (gate_grad, gate_moment))
        load(1, (down_grad, down_moment))

    def wait_loads(slot):
        for member in range(2):
            pltpu.make_async_copy(
                gate_grad, inputs.at[slot, member], input_sem.at[slot, member]
            ).wait()

    def part(block):
        if block < strips:
            return pl.ds(block * BLOCK, BLOCK + (EXTRA if block == strips - 1 else 0))
        return pl.ds(EXTRA + block * BLOCK, BLOCK)

    def near_copy(expert, block):
        row = part(block)
        return pltpu.make_async_remote_copy(
            src_ref=near_send.at[expert, row],
            dst_ref=near_recv.at[expert, row],
            send_sem=near_sems.at[0, expert, block],
            recv_sem=near_sems.at[1, expert, block],
            device_id={"shard": near},
            device_id_type=MESH,
        )

    def far_copy(stage, expert, block):
        row = part(block)
        return pltpu.make_async_remote_copy(
            src_ref=far_send.at[expert, row],
            dst_ref=far_recv.at[stage, expert, row],
            send_sem=far_sems.at[0, stage, expert, block],
            recv_sem=far_sems.at[1, stage, expert, block],
            device_id={"shard": far(stage)},
            device_id_type=MESH,
        )

    def first_copy(expert):
        return pltpu.make_async_remote_copy(
            src_ref=first.at[expert],
            dst_ref=first_other.at[expert],
            send_sem=polished_sems.at[0, expert, blocks],
            recv_sem=polished_sems.at[1, expert, blocks],
            device_id={"shard": near},
            device_id_type=MESH,
        )

    def second_copy(expert, block):
        row = pl.ds(block * BLOCK, BLOCK)
        return pltpu.make_async_remote_copy(
            src_ref=second.at[expert, row],
            dst_ref=other_second.at[expert, row],
            send_sem=polished_sems.at[0, expert, block],
            recv_sem=polished_sems.at[1, expert, block],
            device_id={"shard": near},
            device_id_type=MESH,
        )

    def blend_slot(slot, expert):
        blend[slot, expert] = blended(inputs[slot, 0, expert], inputs[slot, 1, expert])

    def packed_gram(slot, expert, target, ready):
        matrix = blend[slot, expert]
        diagonal = jnp.zeros((1, half), F32)
        row_at, column_at = (at[:BLOCK] for at in iotas(half))
        for block in range(strips):
            start = block * BLOCK
            strip = transposed_product(matrix[:, start : start + BLOCK], matrix)
            last = transposed_product(matrix[:, half + start : half + start + BLOCK], matrix[:, half:])
            target[expert, part(strips + block)] = strip[:, half:].astype(target.dtype)
            target[expert, pl.ds(start, BLOCK)] = jnp.where(
                row_at + start <= column_at, strip[:, :half], last
            ).astype(target.dtype)
            diagonal = diagonal + jnp.sum(
                jnp.where(row_at + start == column_at, last, 0.0), axis=0, keepdims=True
            )
            if block == strips - 1:
                target[expert, pl.ds(half, EXTRA)] = jnp.broadcast_to(diagonal, (EXTRA, half)).astype(
                    target.dtype
                )
            ready(expert, block)
        for block in range(strips, blocks):
            ready(expert, block)

    def enter():
        pl.semaphore_wait(barrier, 1 + stages)

    def send_near(expert, block):
        if experts == 1 and block == 0:
            enter()
        near_copy(expert, block).start()

    def gather_near(expert, block):
        row = part(block)
        near_copy(expert, block).wait_recv()
        held = total[expert, row] + near_recv[expert, row].astype(F32)
        total[expert, row] = held
        if stages:
            far_send[expert, row] = held.astype(BF16)
            far_copy(0, expert, block).start()

    wait_loads(0)
    each(experts, lambda expert: blend_slot(0, expert))
    if experts > 1:
        enter()
    each(experts, lambda expert: packed_gram(0, expert, near_send, send_near))
    wait_loads(1)
    each(experts, lambda expert: blend_slot(1, expert))
    each(experts, lambda expert: packed_gram(1, expert, total, gather_near))

    for stage in range(stages):
        if stage:

            def send_far(expert, stage=stage):
                for block in range(blocks):
                    row = part(block)
                    far_copy(stage - 1, expert, block).wait_send()
                    far_send[expert, row] = total[expert, row].astype(BF16)
                    far_copy(stage, expert, block).start()

            each(experts, send_far)

        def gather_far(expert, block, stage=stage):
            row = part(block)
            far_copy(stage, expert, block).wait_recv()
            held = total[expert, row] + far_recv[stage, expert, row].astype(F32)
            total[expert, row] = held

        def gather_strips(expert, gather_far=gather_far):
            for block in range(blocks):
                gather_far(expert, block)

        if stage < stages - 1:
            each(experts, gather_strips)

    def polish(expert):
        row_at, column_at = iotas(half)
        for block in range(strips if stages else 0):
            gather_far(expert, block)
        packed = total[expert, pl.ds(0, half)]
        diagonal = total[expert, pl.ds(half, 1)]
        kept = jnp.where(row_at == column_at, packed, 0.0)
        trace = jnp.sum(jnp.sum(kept, axis=0, keepdims=True) + diagonal, axis=1, keepdims=True)
        factor = 1.0 / (jnp.sqrt(trace) + EPSILON)
        square = factor * factor
        upper, lower = pl.ds(0, half), pl.ds(half, half)
        packed = packed * square
        flipped = packed.T
        scaled_ref[upper, upper] = jnp.where(row_at <= column_at, packed, flipped).astype(BF16)
        scaled_ref[lower, lower] = jnp.where(
            row_at == column_at,
            diagonal * square,
            jnp.where(row_at > column_at, packed, flipped),
        ).astype(BF16)
        for block in range(strips):
            if stages:
                gather_far(expert, strips + block)
            row = pl.ds(block * BLOCK, BLOCK)
            side = (total[expert, part(strips + block)] * square).astype(BF16)
            scaled_ref[row, lower] = side
            scaled_ref[lower, row] = side.T
        scaled = scaled_ref[...]
        first[expert] = quintic(scaled, product(scaled, scaled), 0).astype(BF16)
        first_copy(expert).start()
        current_ref[...] = product(scaled, first[expert]).astype(BF16)
        scaled_ref[...] = product(first[expert], current_ref[...]).astype(BF16)
        gain = math.sqrt(full_rows) * factor
        for block in range(blocks):
            row = pl.ds(block * BLOCK, BLOCK)
            current = scaled_ref[row]
            step = quintic(current, product(current, scaled_ref[...]), block * BLOCK)
            second[expert, row] = (step * gain).astype(BF16)
            second_copy(expert, block).start()

    each(experts, polish)

    def own_update(expert):
        halfway = product(blend[1, expert], first[expert]).astype(BF16)
        own_out[expert] = product(halfway, second[expert]).astype(BF16)

    each(experts, own_update)

    def other_update(expert):
        first_copy(expert).wait_recv()
        other_half[expert] = product(blend[0, expert], first_other[expert]).astype(BF16)

    each(experts, other_update)

    def drain(expert):
        first_copy(expert).wait_send()
        for block in range(blocks):
            second_copy(expert, block).wait_recv()
            second_copy(expert, block).wait_send()
            near_copy(expert, block).wait_send()
            if stages:
                far_copy(stages - 1, expert, block).wait_send()

    each(experts, drain)


def finish(own, other_half, other_second, gate, down, other, sems):
    experts, rows, _ = own.shape
    core = lax.rem(lax.axis_index("shard"), 2)
    pieces = sems.shape[0] - 1

    def copies(source, target, piece):
        row = pl.ds(0, rows) if piece == pieces else pl.ds(piece * (rows // pieces), rows // pieces)
        return pltpu.make_async_copy(source.at[:, row], target.at[:, row], sems.at[piece])

    def start(source, piece, low, high):
        pl.when(core == 0)(lambda: copies(source, low, piece).start())
        pl.when(core == 1)(lambda: copies(source, high, piece).start())

    start(own, pieces, gate, down)
    for piece in range(pieces):
        row = pl.ds(piece * (rows // pieces), rows // pieces)

        def update(expert, row=row):
            other[expert, row] = product(other_half[expert, row], other_second[expert]).astype(BF16)

        each(experts, update)
        start(other, piece, down, gate)
    for piece in range(pieces + 1):
        copies(other, gate, piece).wait()


def updates(shards, gate_grad, gate_moment, down_grad, down_moment):
    experts, rows, width = gate_grad.shape
    stages = max(shards.bit_length() - 2, 1)
    blocks = width // BLOCK
    packed = (width + EXTRA, width // 2)
    limit = experts * (24 * rows * width + (16 + 2 * stages) * width * width) + (16 << 20)
    own, other_half, other_second = pl.pallas_call(
        functools.partial(kernel, shards, rows * shards),
        out_shape=(
            pltpu.VMEM((experts, rows, width), BF16),
            pltpu.VMEM((experts, rows, width), BF16),
            pltpu.VMEM((experts, width, width), BF16),
        ),
        in_specs=[pl.BlockSpec(memory_space=pltpu.HBM)] * 4,
        out_specs=(pl.BlockSpec(memory_space=pltpu.VMEM),) * 3,
        scratch_shapes=[
            pltpu.VMEM((2, 2, experts, rows, width), BF16),
            pltpu.VMEM((2, experts, rows, width), BF16),
            pltpu.VMEM((experts, *packed), F32),
            pltpu.VMEM((experts, *packed), BF16),
            pltpu.VMEM((experts, *packed), BF16),
            pltpu.VMEM((experts, *packed), BF16),
            pltpu.VMEM((stages, experts, *packed), BF16),
            pltpu.VMEM((width, width), BF16),
            pltpu.VMEM((experts, width, width), BF16),
            pltpu.VMEM((experts, width, width), BF16),
            pltpu.VMEM((experts, width, width), BF16),
            pltpu.VMEM((width, width), BF16),
            pltpu.SemaphoreType.DMA((2, 2)),
            pltpu.SemaphoreType.DMA((2, experts, blocks)),
            pltpu.SemaphoreType.DMA((2, stages, experts, blocks)),
            pltpu.SemaphoreType.DMA((2, experts, blocks + 1)),
        ],
        compiler_params=pltpu.CompilerParams(collective_id=0, has_side_effects=True, vmem_limit_bytes=min(limit, 56 << 20)
        ),
    )(
        *(
            pltpu.with_memory_space_constraint(source, pltpu.HBM)
            for source in (gate_grad, gate_moment, down_grad, down_moment)
        )
    )
    result = jax.ShapeDtypeStruct((experts, rows, width), BF16)
    return pl.pallas_call(
        finish,
        out_shape=(result, result),
        in_specs=[pl.BlockSpec(memory_space=pltpu.VMEM)] * 3,
        out_specs=(pl.BlockSpec(memory_space=pl.ANY),) * 2,
        scratch_shapes=[
            pltpu.VMEM((experts, rows, width), BF16),
            pltpu.SemaphoreType.DMA((3,)),
        ],
        compiler_params=pltpu.CompilerParams(vmem_limit_bytes=8 << 20),
    )(own, other_half, other_second)


def solution(mesh):
    placed = P("layer", "shard", None)
    return jax.shard_map(
        functools.partial(updates, mesh.shape["shard"]),
        mesh=mesh,
        in_specs=(placed,) * 4,
        out_specs=(placed,) * 2,
        check_vma=False,
    )
```
